512 devices in a mesh: surf: 512 (over x, z, y, core).
Axes of the slice: x: 4, y: 4, z: 16, core: 2. Of those that a mesh axis runs over, the one named last changes fastest.
Arguments:
- excitation: float32 [2, 262144, 256], P(None, 'surf'), may hold values from -6 to 6
- leaf_basis: bfloat16 [2, 131072, 512], P(None, 'surf'), may hold values from -0.1875 to 0.1875
- self_transfer: bfloat16 [3, 2, 131072, 256], P(None, None, 'surf'), may hold values from -0.1875 to 0.1875
- cross_transfer: bfloat16 [3, 2, 131072, 256], P(None, None, 'surf'), may hold values from -0.1875 to 0.1875
- out_basis: bfloat16 [2, 262144, 256], P(None, 'surf'), may hold values from -0.25 to 0.25
- near_tiles: bfloat16 [3072, 2, 128, 128], P('surf'), may hold values from -0.375 to 0.375
- near_list: int32 [512, 6, 3], replicated, may hold values from -1 to 511, as said below
Outputs:
- response: float32 [2, 262144, 256], P(None, 'surf')
The draws below stay inside these ranges and needn't reach their ends.
Inputs may be any that keep to these rules, and one draw needn't show every extreme that they name: `near_list`: row i lists patch i's near tiles as (owner, row tile, column tile). An owner is i - 1, i or i + 1 modulo 512, or -1 for an empty slot; empty slots come last and hold 0 for both tiles. Every patch has at least one tile and some patch fills all 6 slots. From one neighbouring patch a patch lists at most 2 distinct column tiles, and some patch reaches 2.
All inputs are finite; a program needn't handle non-finite values.
Results may differ from the reference program's by a relative error of at most 0.0051.
Values may be sent and summed in bfloat16 or wider, within the bound.
A program may use at most 64 MiB of HBM per device.

```python
import jax
import jax.numpy as jnp
from jax import lax

TILE = 128
PATCH_ROW_TILES = 4
RANK = 256
COLS = 256
BUTTERFLY_DEPTH = 3
NEAR_TILE_SLOTS = 6
ROWS = 512
ORDER = 262144
N_SURF = 512


def draw_near_list(key, part):
    random_keys = jax.random.split(jax.random.fold_in(key, 71), 7)
    processor_index = jnp.arange(N_SURF, dtype=jnp.int32)[:, None]
    transfer_group = jax.random.randint(random_keys[0], (N_SURF,), 0, 8) == 0
    tile_count = jnp.where(transfer_group, NEAR_TILE_SLOTS, jax.random.randint(random_keys[1], (N_SURF,), min(4, NEAR_TILE_SLOTS), NEAR_TILE_SLOTS + 1))
    tile_count = tile_count.at[0].set(NEAR_TILE_SLOTS)
    first = jax.random.randint(random_keys[2], (N_SURF, 3), 0, PATCH_ROW_TILES)
    second = (first + jax.random.randint(random_keys[3], (N_SURF, 3), 1, PATCH_ROW_TILES)) % PATCH_ROW_TILES
    draw_side = jax.random.randint(random_keys[4], (N_SURF, NEAR_TILE_SLOTS), 0, 5)
    side = jnp.where(draw_side < 2, 0, jnp.where(draw_side == 2, 1, 2))
    side = side.at[0, 0].set(2).at[0, 1].set(2)
    pick = jax.random.randint(random_keys[5], (N_SURF, NEAR_TILE_SLOTS), 0, 2)
    pick = pick.at[0, 0].set(0).at[0, 1].set(1)
    column = jnp.where(pick == 0, jnp.take_along_axis(first, side, 1), jnp.take_along_axis(second, side, 1))
    row_tile = jax.random.randint(random_keys[6], (N_SURF, NEAR_TILE_SLOTS), 0, PATCH_ROW_TILES)
    owner = (processor_index + side - 1) % N_SURF
    live = jnp.arange(NEAR_TILE_SLOTS)[None, :] < tile_count[:, None]
    owner = jnp.where(live, owner, -1)
    row_tile = jnp.where(live, row_tile, 0)
    column = jnp.where(live, column, 0)
    return jnp.stack([owner, row_tile, column], -1).astype(jnp.int32)


def block_levels(rng, shape, cuts, smallest, high):
    def one(dim, parts):
        steps = jax.random.uniform(jax.random.fold_in(jax.random.fold_in(rng, 6), dim), (parts,), jnp.float32, smallest / len(cuts), high / len(cuts))
        return jnp.repeat(jnp.exp(steps), shape[dim] // parts).reshape((-1,) + (1,) * (len(shape) - dim - 1))

    factor_of = one(*cuts[0])
    for cut in cuts[1:]:
        factor_of = factor_of * one(*cut)
    return factor_of


def bell_draw(rng, shape, spread, limit, cuts=(), kind=jnp.bfloat16):
    level = block_levels(rng, shape, cuts, -0.22, 0.18) if cuts else 1.0
    drawn = jax.random.normal(rng, shape, jnp.float32) * spread * level
    return jnp.minimum(jnp.maximum(drawn, -limit), limit).astype(kind)


def setup_inputs(seed: int = 0) -> dict:
    splits = jax.random.split(jax.random.key(seed), 8)
    excitation = bell_draw(splits[0], (2, ORDER, COLS), 1.0, 6.0, ((1, 512),), jnp.float32)
    leaf_basis = bell_draw(splits[1], (2, RANK * N_SURF, ROWS), (2 * ROWS) ** -0.5, 0.1875, ((1, 512),))
    self_transfer = bell_draw(splits[2], (BUTTERFLY_DEPTH, 2, RANK * N_SURF, RANK), (4 * RANK) ** -0.5, 0.1875, ((2, 512),))
    cross_transfer = bell_draw(splits[3], (BUTTERFLY_DEPTH, 2, RANK * N_SURF, RANK), (4 * RANK) ** -0.5, 0.1875, ((2, 512),))
    out_basis = bell_draw(splits[4], (2, ORDER, RANK), (2 * RANK) ** -0.5, 0.25, ((1, 512),))
    near_tiles = bell_draw(splits[5], (N_SURF * NEAR_TILE_SLOTS, 2, TILE, TILE), (2 * TILE) ** -0.5, 0.375, ((0, 512),))
    near_list = draw_near_list(jax.random.fold_in(splits[7], 71), 0)
    return dict(excitation=excitation, leaf_basis=leaf_basis, self_transfer=self_transfer, cross_transfer=cross_transfer, out_basis=out_basis, near_tiles=near_tiles, near_list=near_list)


def cmat(matrix, vector):
    real = jnp.dot(matrix[0], vector[0], preferred_element_type=jnp.float32) - jnp.dot(matrix[1], vector[1], preferred_element_type=jnp.float32)
    imag = jnp.dot(matrix[0], vector[1], preferred_element_type=jnp.float32) + jnp.dot(matrix[1], vector[0], preferred_element_type=jnp.float32)
    return jnp.stack([real, imag])


def per_patch(array, inner, last):
    return array.reshape(2, N_SURF, inner, last).transpose(1, 0, 2, 3)


def reference(excitation, leaf_basis, self_transfer, cross_transfer, out_basis, near_tiles, near_list):
    xb = excitation.astype(jnp.bfloat16)
    patches = per_patch(xb, ROWS, COLS)
    leaves = per_patch(leaf_basis, RANK, ROWS)
    coef = lax.map(lambda pair: cmat(pair[0], pair[1]).astype(jnp.bfloat16), (leaves, patches))
    idents = jnp.arange(N_SURF, dtype=jnp.int32)
    for level in range(BUTTERFLY_DEPTH):
        exchange_partner = coef[jnp.bitwise_xor(idents, 1 << level)]
        own_maps = per_patch(self_transfer[level], RANK, RANK)
        far_maps = per_patch(cross_transfer[level], RANK, RANK)
        coef = lax.map(lambda quad: (cmat(quad[0], quad[1]) + cmat(quad[2], quad[3])).astype(jnp.bfloat16), (own_maps, coef, far_maps, exchange_partner))
    outs = per_patch(out_basis, ROWS, RANK)
    far = lax.map(lambda pair: cmat(pair[0], pair[1]), (outs, coef))
    tiles = near_tiles.reshape(N_SURF, NEAR_TILE_SLOTS, 2, TILE, TILE)
    block_ids = jnp.arange(PATCH_ROW_TILES, dtype=jnp.int32)

    def near_one(pair):
        tile_set, listing = pair
        near = jnp.zeros((2, PATCH_ROW_TILES, TILE, COLS), jnp.float32)
        for slot in range(NEAR_TILE_SLOTS):
            owner = listing[slot, 0]
            valid = (owner >= 0).astype(jnp.float32)
            start = (jnp.maximum(owner, 0) * ROWS + listing[slot, 2] * TILE).astype(jnp.int32)
            block = lax.dynamic_slice_in_dim(xb, start, TILE, 1)
            term = cmat(tile_set[slot], block) * valid
            hit = (block_ids == listing[slot, 1].astype(jnp.int32)).astype(jnp.float32)
            near = near + term[:, None] * hit[None, :, None, None]
        return near.reshape(2, ROWS, COLS)

    near = lax.map(near_one, (tiles, near_list))
    total = far + near
    return total.transpose(1, 0, 2, 3).reshape(2, N_SURF * ROWS, COLS)
```

```python
import functools

import jax
import jax.numpy as jnp
from jax import lax
from jax.experimental import pallas as pl
from jax.experimental.pallas import tpu as pltpu
from jax.sharding import PartitionSpec as P

MESH = pl.DeviceIdType.MESH
CHUNKS = 2


def cmul(real, imag, block):
    half = block.shape[-1] // 2
    turned = jnp.concatenate([-block[:, half:], block[:, :half]], axis=1)
    return jnp.dot(real, block, preferred_element_type=jnp.float32) + jnp.dot(
        imag, turned, preferred_element_type=jnp.float32
    )


def kernel(
    n,
    x_hbm,
    leaf_hbm,
    self_hbm,
    cross_hbm,
    out_hbm,
    tiles_hbm,
    list_hbm,
    o_hbm,
    xf,
    xb,
    window,
    leaf,
    own,
    cross,
    outb,
    tiles,
    listed,
    near_send,
    near_recv,
    coef,
    got,
    terms,
    near,
    ostage,
    load_sem,
    near_ssem,
    near_rsem,
    send_sem,
    recv_sem,
    store_sem,
):
    me = lax.axis_index("surf")
    left = lax.rem(me + n - 1, n)
    right = lax.rem(me + 1, n)
    levels = own.shape[0]
    blocks, tile, wide = xb.shape
    width = wide // 2
    part = width // CHUNKS
    slots = tiles.shape[0]

    barrier = pltpu.get_barrier_semaphore()
    peers = [left, right] + [me ^ (1 << l) for l in range(levels)]
    for peer in peers:
        pl.semaphore_signal(barrier, inc=1, device_id=(peer,), device_id_type=MESH)

    loads = {}

    def load(name, src, dst):
        loads[name] = pltpu.make_async_copy(src, dst, load_sem.at[len(loads)])
        loads[name].start()

    load("x", x_hbm, xf)
    load("leaf", leaf_hbm, leaf)
    load("list", list_hbm, listed)
    for l in range(levels):
        load(f"self{l}", self_hbm.at[l], own.at[l])
        load(f"cross{l}", cross_hbm.at[l], cross.at[l])
    load("tiles", tiles_hbm, tiles)
    load("out", out_hbm, outb)

    loads["x"].wait()
    for b in range(blocks):
        rows = slice(b * tile, (b + 1) * tile)
        both = jnp.concatenate([xf[0, rows, :], xf[1, rows, :]], axis=1).astype(jnp.bfloat16)
        xb[b] = both
        window[b] = both

    def chunk(c):
        lo, hi = c * part, (c + 1) * part
        rows = blocks * tile
        real = xb[:, :, lo:hi].reshape(rows, part)
        imag = xb[:, :, width + lo : width + hi].reshape(rows, part)
        return jnp.concatenate([real, imag], axis=1)

    def exchange(level, c):
        return pltpu.make_async_remote_copy(
            src_ref=coef.at[level, c],
            dst_ref=got.at[level, c],
            send_sem=send_sem.at[level, c],
            recv_sem=recv_sem.at[level, c],
            device_id=(me ^ (1 << level),),
            device_id_type=MESH,
        )

    loads["list"].wait()

    def listed_span(patch, owner):
        low, high = jnp.int32(blocks), jnp.int32(-1)
        for k in range(slots):
            hit = listed[k, 0, patch] == owner
            col = listed[k, 2, patch]
            low = jnp.minimum(low, jnp.where(hit, col, blocks))
            high = jnp.maximum(high, jnp.where(hit, col, -1))
        return jnp.where(high < 0, 0, low), jnp.maximum(high, 0)

    pl.semaphore_wait(barrier, len(peers))
    near_copies = []
    for s, (patch, landing) in enumerate(((left, 1), (right, 0))):
        low, high = listed_span(patch, me)
        near_send[s, 0] = xb[low]
        near_send[s, 1] = xb[high]
        copy = pltpu.make_async_remote_copy(
            src_ref=near_send.at[s],
            dst_ref=near_recv.at[landing],
            send_sem=near_ssem.at[s],
            recv_sem=near_rsem.at[landing],
            device_id=(patch,),
            device_id_type=MESH,
        )
        copy.start()
        near_copies.append(copy)

    loads["leaf"].wait()
    copies = {}
    for c in range(CHUNKS):
        coef[0, c] = cmul(leaf[0], leaf[1], chunk(c)).astype(jnp.bfloat16)
        copies[0, c] = exchange(0, c)
        copies[0, c].start()

    def near_field():
        loads["tiles"].wait()
        for copy in near_copies:
            copy.wait_recv()
        for s in range(2):
            for h in range(2):
                window[blocks + 2 * s + h] = near_recv[s, h]
        low_left, _ = listed_span(me, left)
        low_right, _ = listed_span(me, right)
        hits = []
        for k in range(slots):
            owner, row, col = listed[k, 0, me], listed[k, 1, me], listed[k, 2, me]
            place = jnp.where(
                owner == left,
                blocks + (col != low_left).astype(jnp.int32),
                jnp.where(owner == right, blocks + 2 + (col != low_right).astype(jnp.int32), col),
            )
            hits.append(jnp.where(owner >= 0, row, -1))
            terms[k] = cmul(tiles[k, 0], tiles[k, 1], window[place])
        for r in range(blocks):
            total = jnp.zeros((tile, wide), jnp.float32)
            for k in range(slots):
                total = total + terms[k] * jnp.where(hits[k] == r, 1.0, 0.0)
            near[r * tile : (r + 1) * tile, :] = total

    stores = []
    for l in range(levels):
        loads[f"self{l}"].wait()
        sums = [cmul(own[l, 0], own[l, 1], coef[l, c]) for c in range(CHUNKS)]
        if l == 1:
            near_field()
        loads[f"cross{l}"].wait()
        for c in range(CHUNKS):
            copies[l, c].wait_recv()
            after = (sums[c] + cmul(cross[l, 0], cross[l, 1], got[l, c])).astype(jnp.bfloat16)
            if l + 1 < levels:
                coef[l + 1, c] = after
                copies[l + 1, c] = exchange(l + 1, c)
                copies[l + 1, c].start()
                continue
            if c == 0:
                loads["out"].wait()
            far = cmul(outb[0], outb[1], after)
            lo, hi = c * part, (c + 1) * part
            ostage[0, :, lo:hi] = far[:, :part] + near[:, lo:hi]
            ostage[1, :, lo:hi] = far[:, part:] + near[:, width + lo : width + hi]
            store = pltpu.make_async_copy(
                ostage.at[:, :, lo:hi], o_hbm.at[:, :, lo:hi], store_sem.at[c]
            )
            store.start()
            stores.append(store)
    for copy in near_copies:
        copy.wait_send()
    for copy in copies.values():
        copy.wait_send()
    for store in stores:
        store.wait()


def per_device(
    excitation, leaf_basis, self_transfer, cross_transfer, out_basis, near_tiles, near_list
):
    n = lax.axis_size("surf")
    rows, width = excitation.shape[1:]
    rank = leaf_basis.shape[1]
    levels = self_transfer.shape[0]
    slots, _, tile, _ = near_tiles.shape
    blocks = rows // tile
    by_slot = jnp.transpose(near_list, (1, 2, 0))
    half, full = jnp.bfloat16, jnp.float32
    anywhere = pl.BlockSpec(memory_space=pl.ANY)
    part = 2 * width // CHUNKS
    return pl.pallas_call(
        functools.partial(kernel, n),
        out_shape=jax.ShapeDtypeStruct(excitation.shape, full),
        in_specs=[anywhere] * 7,
        out_specs=anywhere,
        scratch_shapes=[
            pltpu.VMEM(excitation.shape, full),
            pltpu.VMEM((blocks, tile, 2 * width), half),
            pltpu.VMEM((blocks + 4, tile, 2 * width), half),
            pltpu.VMEM(leaf_basis.shape, half),
            pltpu.VMEM(self_transfer.shape, half),
            pltpu.VMEM(cross_transfer.shape, half),
            pltpu.VMEM(out_basis.shape, half),
            pltpu.VMEM(near_tiles.shape, half),
            pltpu.SMEM(by_slot.shape, jnp.int32),
            pltpu.VMEM((2, 2, tile, 2 * width), half),
            pltpu.VMEM((2, 2, tile, 2 * width), half),
            pltpu.VMEM((levels, CHUNKS, rank, part), half),
            pltpu.VMEM((levels, CHUNKS, rank, part), half),
            pltpu.VMEM((slots, tile, 2 * width), full),
            pltpu.VMEM((rows, 2 * width), full),
            pltpu.VMEM(excitation.shape, full),
            pltpu.SemaphoreType.DMA((5 + 2 * levels,)),
            pltpu.SemaphoreType.DMA((2,)),
            pltpu.SemaphoreType.DMA((2,)),
            pltpu.SemaphoreType.DMA((levels, CHUNKS)),
            pltpu.SemaphoreType.DMA((levels, CHUNKS)),
            pltpu.SemaphoreType.DMA((CHUNKS,)),
        ],
        compiler_params=pltpu.CompilerParams(collective_id=0, has_side_effects=True),
    )(
        excitation,
        leaf_basis,
        self_transfer,
        cross_transfer,
        out_basis,
        near_tiles,
        by_slot,
    )


def solution(mesh):
    placed = (
        P(None, "surf", None),
        P(None, "surf", None),
        P(None, None, "surf", None),
        P(None, None, "surf", None),
        P(None, "surf", None),
        P("surf", None, None, None),
        P(),
    )
    return jax.shard_map(
        per_device, mesh=mesh, in_specs=placed, out_specs=P(None, "surf", None), check_vma=False
    )
```

```python
import functools

import jax
import jax.numpy as jnp
from jax import lax
from jax.experimental import pallas as pl
from jax.experimental.pallas import tpu as pltpu
from jax.sharding import PartitionSpec as P

MESH = pl.DeviceIdType.MESH
CHUNKS = 2


def cmul(real, imag, block):
    half = block.shape[-1] // 2
    plain = jnp.dot(real, block, preferred_element_type=jnp.float32)
    if half % 128 == 0:
        turned = jnp.concatenate([-block[:, half:], block[:, :half]], axis=1)
        return plain + jnp.dot(imag, turned, preferred_element_type=jnp.float32)
    other = pltpu.roll(jnp.dot(imag, block, preferred_element_type=jnp.float32), half, 1)
    lane = lax.broadcasted_iota(jnp.int32, other.shape, 1)
    return plain + jnp.where(lane < half, -other, other)


def kernel(
    n,
    x_hbm,
    leaf_hbm,
    self_hbm,
    cross_hbm,
    out_hbm,
    tiles_hbm,
    list_hbm,
    o_ref,
    xf,
    xb,
    window,
    leaf,
    own,
    cross,
    outb,
    tiles,
    listed,
    near_send,
    near_recv,
    coef,
    got,
    terms,
    near,
    load_sem,
    near_ssem,
    near_rsem,
    send_sem,
    recv_sem,
    ready,
):
    me = lax.axis_index("surf")
    levels = own.shape[0]
    blocks, tile, wide = xb.shape
    width = wide // 2
    part = width // CHUNKS
    slots = tiles.shape[0]
    group = 1 << levels

    def parity(device):
        return lax.rem(sum(lax.rem(device // (1 << l), 2) for l in range(levels)), 2)

    odd = lax.rem(me, 2)
    left = lax.rem(me + n - 1, n)
    right = lax.rem(me + 1, n)
    mate = me ^ 1
    beside = lax.rem(me + n - 1 + 2 * odd, n)
    place = lax.rem(me, group)
    last_side = levels
    hub = parity(me) == 0
    answers_beside = jnp.where(parity(me) != parity(beside), parity(me) == 0, odd == 1)
    barrier = pltpu.get_barrier_semaphore()

    def greet(device):
        pl.semaphore_signal(barrier, inc=1, device_id=(device,), device_id_type=MESH)

    def answer(device, which):
        pl.semaphore_signal(ready.at[which], inc=1, device_id=(device,), device_id_type=MESH)

    @pl.when(jnp.logical_not(hub))
    def _():
        for l in range(levels):
            greet(me ^ (1 << l))

    @pl.when(jnp.logical_not(answers_beside))
    def _():
        greet(beside)

    loads = {}

    def load(name, src, dst):
        loads[name] = pltpu.make_async_copy(src, dst, load_sem.at[len(loads)])
        loads[name].start()

    load("x", x_hbm, xf)
    load("leaf", leaf_hbm, leaf)
    load("list", list_hbm, listed)
    for l in range(levels):
        load(f"self{l}", self_hbm.at[l], own.at[l])
        load(f"cross{l}", cross_hbm.at[l], cross.at[l])
    load("tiles", tiles_hbm, tiles)
    load("out", out_hbm, outb)

    @pl.when(jnp.logical_and(hub, answers_beside))
    def _():
        pl.semaphore_wait(barrier, levels + 1)

    @pl.when(jnp.logical_and(hub, jnp.logical_not(answers_beside)))
    def _():
        pl.semaphore_wait(barrier, levels)

    @pl.when(jnp.logical_and(jnp.logical_not(hub), answers_beside))
    def _():
        pl.semaphore_wait(barrier, 1)

    @pl.when(hub)
    def _():
        for l in range(levels):
            answer(me ^ (1 << l), l)

    @pl.when(answers_beside)
    def _():
        answer(beside, last_side)

    def until_ready(level):
        @pl.when(jnp.logical_not(hub))
        def _():
            pl.semaphore_wait(ready.at[level], 1)

    loads["x"].wait()
    for b in range(blocks):
        rows = slice(b * tile, (b + 1) * tile)
        both = jnp.concatenate([xf[0, rows, :], xf[1, rows, :]], axis=1).astype(jnp.bfloat16)
        xb[b] = both
        window[b] = both

    def chunk(c):
        lo, hi = c * part, (c + 1) * part
        rows = blocks * tile
        real = xb[:, :, lo:hi].reshape(rows, part)
        imag = xb[:, :, width + lo : width + hi].reshape(rows, part)
        return jnp.concatenate([real, imag], axis=1)

    def exchange(level, c):
        return pltpu.make_async_remote_copy(
            src_ref=coef.at[level, c],
            dst_ref=got.at[level, c],
            send_sem=send_sem.at[level, c],
            recv_sem=recv_sem.at[level, c],
            device_id=(me ^ (1 << level),),
            device_id_type=MESH,
        )

    def listed_span(patch, owner):
        low, high = jnp.int32(blocks), jnp.int32(-1)
        for k in range(slots):
            hit = listed[k, 0, patch] == owner
            col = listed[k, 2, patch]
            low = jnp.minimum(low, jnp.where(hit, col, blocks))
            high = jnp.maximum(high, jnp.where(hit, col, -1))
        return jnp.where(high < 0, 0, low), jnp.maximum(high, 0)

    def near_copy(side, device):
        return pltpu.make_async_remote_copy(
            src_ref=near_send.at[side],
            dst_ref=near_recv.at[side],
            send_sem=near_ssem.at[side],
            recv_sem=near_rsem.at[side],
            device_id=(device,),
            device_id_type=MESH,
        )

    near_copies = [near_copy(0, mate), near_copy(1, beside)]

    def send_near(side, device):
        low, high = listed_span(device, me)
        near_send[side, 0] = xb[low]
        near_send[side, 1] = xb[high]
        near_copies[side].start()

    def send_beside(when):
        @pl.when(when)
        def _():
            @pl.when(jnp.logical_not(answers_beside))
            def _():
                pl.semaphore_wait(ready.at[last_side], 1)

            send_near(1, beside)

    first, last = place == 0, place == group - 1
    loads["list"].wait()
    send_beside(jnp.logical_not(jnp.logical_or(first, last)))

    loads["leaf"].wait()
    copies = {}
    for c in range(CHUNKS):
        coef[0, c] = cmul(leaf[0], leaf[1], chunk(c)).astype(jnp.bfloat16)
        copies[0, c] = exchange(0, c)
        if c == 0:
            until_ready(0)
        copies[0, c].start()
    send_near(0, mate)

    def near_field():
        loads["tiles"].wait()
        for copy in near_copies:
            copy.wait_recv()
        for s in range(2):
            for h in range(2):
                window[blocks + 2 * s + h] = near_recv[s, h]
        low_mate, _ = listed_span(me, mate)
        low_beside, _ = listed_span(me, beside)
        hits = []
        for k in range(slots):
            owner, row, col = listed[k, 0, me], listed[k, 1, me], listed[k, 2, me]
            at = jnp.where(
                owner == mate,
                blocks + (col != low_mate).astype(jnp.int32),
                jnp.where(owner == beside, blocks + 2 + (col != low_beside).astype(jnp.int32), col),
            )
            hits.append(jnp.where(owner >= 0, row, -1))
            terms[k] = cmul(tiles[k, 0], tiles[k, 1], window[at])
        for r in range(blocks):
            total = jnp.zeros((tile, wide), jnp.float32)
            for k in range(slots):
                total = total + terms[k] * jnp.where(hits[k] == r, 1.0, 0.0)
            near[r * tile : (r + 1) * tile, :] = total

    for l in range(levels):
        loads[f"self{l}"].wait()
        sums = [cmul(own[l, 0], own[l, 1], coef[l, c]) for c in range(CHUNKS)]
        if l == 1:
            send_beside(first)
        if l + 1 == levels:
            send_beside(last)
            near_field()
        loads[f"cross{l}"].wait()
        for c in range(CHUNKS):
            copies[l, c].wait_recv()
            after = (sums[c] + cmul(cross[l, 0], cross[l, 1], got[l, c])).astype(jnp.bfloat16)
            if l + 1 < levels:
                coef[l + 1, c] = after
                copies[l + 1, c] = exchange(l + 1, c)
                if c == 0:
                    until_ready(l + 1)
                copies[l + 1, c].start()
                continue
            if c == 0:
                loads["out"].wait()
            far = cmul(outb[0], outb[1], after)
            lo, hi = c * part, (c + 1) * part
            o_ref[0, :, lo:hi] = far[:, :part] + near[:, lo:hi]
            o_ref[1, :, lo:hi] = far[:, part:] + near[:, width + lo : width + hi]
    for copy in near_copies:
        copy.wait_send()
    for copy in copies.values():
        copy.wait_send()


def per_device(
    excitation, leaf_basis, self_transfer, cross_transfer, out_basis, near_tiles, near_list
):
    n = lax.axis_size("surf")
    rows, width = excitation.shape[1:]
    rank = leaf_basis.shape[1]
    levels = self_transfer.shape[0]
    slots, _, tile, _ = near_tiles.shape
    blocks = rows // tile
    by_slot = jnp.transpose(near_list, (1, 2, 0))
    half, full = jnp.bfloat16, jnp.float32
    anywhere = pl.BlockSpec(memory_space=pl.ANY)
    part = 2 * width // CHUNKS
    return pl.pallas_call(
        functools.partial(kernel, n),
        out_shape=pltpu.VMEM(excitation.shape, full),
        in_specs=[anywhere] * 7,
        out_specs=pl.BlockSpec(memory_space=pltpu.VMEM),
        scratch_shapes=[
            pltpu.VMEM(excitation.shape, full),
            pltpu.VMEM((blocks, tile, 2 * width), half),
            pltpu.VMEM((blocks + 4, tile, 2 * width), half),
            pltpu.VMEM(leaf_basis.shape, half),
            pltpu.VMEM(self_transfer.shape, half),
            pltpu.VMEM(cross_transfer.shape, half),
            pltpu.VMEM(out_basis.shape, half),
            pltpu.VMEM(near_tiles.shape, half),
            pltpu.SMEM(by_slot.shape, jnp.int32),
            pltpu.VMEM((2, 2, tile, 2 * width), half),
            pltpu.VMEM((2, 2, tile, 2 * width), half),
            pltpu.VMEM((levels, CHUNKS, rank, part), half),
            pltpu.VMEM((levels, CHUNKS, rank, part), half),
            pltpu.VMEM((slots, tile, 2 * width), full),
            pltpu.VMEM((rows, 2 * width), full),
            pltpu.SemaphoreType.DMA((5 + 2 * levels,)),
            pltpu.SemaphoreType.DMA((2,)),
            pltpu.SemaphoreType.DMA((2,)),
            pltpu.SemaphoreType.DMA((levels, CHUNKS)),
            pltpu.SemaphoreType.DMA((levels, CHUNKS)),
            pltpu.SemaphoreType.REGULAR((levels + 1,)),
        ],
        compiler_params=pltpu.CompilerParams(
            collective_id=0, has_side_effects=True, vmem_limit_bytes=24 << 20
        ),
    )(
        *(
            pltpu.with_memory_space_constraint(array, pltpu.HBM)
            for array in (
                excitation,
                leaf_basis,
                self_transfer,
                cross_transfer,
                out_basis,
                near_tiles,
                by_slot,
            )
        )
    )


def solution(mesh):
    placed = (
        P(None, "surf", None),
        P(None, "surf", None),
        P(None, None, "surf", None),
        P(None, None, "surf", None),
        P(None, "surf", None),
        P("surf", None, None, None),
        P(),
    )
    return jax.shard_map(
        per_device, mesh=mesh, in_specs=placed, out_specs=P(None, "surf", None), check_vma=False
    )
```

```python
import functools

import jax
import jax.numpy as jnp
from jax import lax
from jax.experimental import pallas as pl
from jax.experimental.pallas import tpu as pltpu
from jax.sharding import PartitionSpec as P

MESH = pl.DeviceIdType.MESH
CHUNKS = 2
SHEET = 128


def cmul(real, imag, block):
    half = block.shape[-1] // 2
    plain = jnp.dot(real, block, preferred_element_type=jnp.float32)
    if half % 128 == 0:
        turned = jnp.concatenate([-block[:, half:], block[:, :half]], axis=1)
        return plain + jnp.dot(imag, turned, preferred_element_type=jnp.float32)
    other = pltpu.roll(jnp.dot(imag, block, preferred_element_type=jnp.float32), half, 1)
    lane = lax.broadcasted_iota(jnp.int32, other.shape, 1)
    return plain + jnp.where(lane < half, -other, other)


def kernel(
    n,
    x_hbm,
    leaf_hbm,
    self_hbm,
    cross_hbm,
    out_hbm,
    tiles_hbm,
    list_hbm,
    o_ref,
    xf,
    xb,
    window,
    leaf,
    own,
    cross,
    outb,
    tiles,
    listed,
    near_send,
    near_recv,
    coef,
    got,
    terms,
    near,
    load_sem,
    near_ssem,
    near_rsem,
    send_sem,
    recv_sem,
    ready,
):
    me = lax.axis_index("surf")
    levels = own.shape[0]
    blocks, tile, wide = xb.shape
    width = wide // 2
    part = width // CHUNKS
    slots = tiles.shape[0]
    group = 1 << levels

    def parity(device):
        return lax.rem(sum(lax.rem(device // (1 << l), 2) for l in range(levels)), 2)

    odd = lax.rem(me, 2)
    left = lax.rem(me + n - 1, n)
    right = lax.rem(me + 1, n)
    mate = me ^ 1
    beside = lax.rem(me + n - 1 + 2 * odd, n)
    place = lax.rem(me, group)
    last_side = levels
    hub = parity(me) == 0
    answers_beside = odd == 1
    barrier = pltpu.get_barrier_semaphore()

    def greet(device):
        pl.semaphore_signal(barrier, inc=1, device_id=(device,), device_id_type=MESH)

    def answer(device, which):
        pl.semaphore_signal(ready.at[which], inc=1, device_id=(device,), device_id_type=MESH)

    @pl.when(jnp.logical_not(hub))
    def _():
        for l in range(levels):
            greet(me ^ (1 << l))

    @pl.when(jnp.logical_not(answers_beside))
    def _():
        greet(beside)

    loads = {}

    def load(name, src, dst):
        loads[name] = pltpu.make_async_copy(src, dst, load_sem.at[len(loads)])
        loads[name].start()

    load("x", x_hbm, xf)
    load("leaf", leaf_hbm, leaf)
    load("list", list_hbm, listed)
    for l in range(levels):
        load(f"self{l}", self_hbm.at[l], own.at[l])
        load(f"cross{l}", cross_hbm.at[l], cross.at[l])
    load("tiles", tiles_hbm, tiles)
    load("out", out_hbm, outb)

    @pl.when(jnp.logical_and(hub, answers_beside))
    def _():
        pl.semaphore_wait(barrier, levels + 1)

    @pl.when(jnp.logical_and(hub, jnp.logical_not(answers_beside)))
    def _():
        pl.semaphore_wait(barrier, levels)

    @pl.when(jnp.logical_and(jnp.logical_not(hub), answers_beside))
    def _():
        pl.semaphore_wait(barrier, 1)

    @pl.when(hub)
    def _():
        for l in range(levels):
            answer(me ^ (1 << l), l)

    @pl.when(answers_beside)
    def _():
        answer(beside, last_side)

    def until_ready(level):
        @pl.when(jnp.logical_not(hub))
        def _():
            pl.semaphore_wait(ready.at[level], 1)

    loads["x"].wait()
    for b in range(blocks):
        rows = slice(b * tile, (b + 1) * tile)
        both = jnp.concatenate([xf[0, rows, :], xf[1, rows, :]], axis=1).astype(jnp.bfloat16)
        xb[b] = both
        window[b] = both

    def chunk(c):
        lo, hi = c * part, (c + 1) * part
        rows = blocks * tile
        real = xb[:, :, lo:hi].reshape(rows, part)
        imag = xb[:, :, width + lo : width + hi].reshape(rows, part)
        return jnp.concatenate([real, imag], axis=1)

    def exchange(level, c):
        return pltpu.make_async_remote_copy(
            src_ref=coef.at[level, c],
            dst_ref=got.at[level, c],
            send_sem=send_sem.at[level, c],
            recv_sem=recv_sem.at[level, c],
            device_id=(me ^ (1 << level),),
            device_id_type=MESH,
        )

    def listed_span(patch, owner):
        low, high = jnp.int32(blocks), jnp.int32(-1)
        for k in range(slots):
            hit = listed[k, 0, patch] == owner
            col = listed[k, 2, patch]
            low = jnp.minimum(low, jnp.where(hit, col, blocks))
            high = jnp.maximum(high, jnp.where(hit, col, -1))
        return jnp.where(high < 0, 0, low), jnp.maximum(high, 0)

    def near_copy(side, device):
        return pltpu.make_async_remote_copy(
            src_ref=near_send.at[side],
            dst_ref=near_recv.at[side],
            send_sem=near_ssem.at[side],
            recv_sem=near_rsem.at[side],
            device_id=(device,),
            device_id_type=MESH,
        )

    near_copies = [near_copy(0, mate), near_copy(1, beside)]

    def send_near(side, device):
        low, high = listed_span(device, me)
        near_send[side, 0] = xb[low]
        near_send[side, 1] = xb[high]
        near_copies[side].start()

    def send_beside(when):
        @pl.when(when)
        def _():
            @pl.when(jnp.logical_not(answers_beside))
            def _():
                pl.semaphore_wait(ready.at[last_side], 1)

            send_near(1, beside)

    first = place == 0
    edge = lax.rem(me, SHEET) == 0
    loads["list"].wait()
    send_beside(jnp.logical_not(first))

    loads["leaf"].wait()
    copies = {}
    for c in range(CHUNKS):
        coef[0, c] = cmul(leaf[0], leaf[1], chunk(c)).astype(jnp.bfloat16)
        copies[0, c] = exchange(0, c)
        if c == 0:
            until_ready(0)
        copies[0, c].start()
    send_near(0, mate)
    send_beside(jnp.logical_and(first, jnp.logical_not(edge)))

    def near_field():
        loads["tiles"].wait()
        for copy in near_copies:
            copy.wait_recv()
        for s in range(2):
            for h in range(2):
                window[blocks + 2 * s + h] = near_recv[s, h]
        low_mate, _ = listed_span(me, mate)
        low_beside, _ = listed_span(me, beside)
        hits = []
        for k in range(slots):
            owner, row, col = listed[k, 0, me], listed[k, 1, me], listed[k, 2, me]
            at = jnp.where(
                owner == mate,
                blocks + (col != low_mate).astype(jnp.int32),
                jnp.where(owner == beside, blocks + 2 + (col != low_beside).astype(jnp.int32), col),
            )
            hits.append(jnp.where(owner >= 0, row, -1))
            terms[k] = cmul(tiles[k, 0], tiles[k, 1], window[at])
        for r in range(blocks):
            total = jnp.zeros((tile, wide), jnp.float32)
            for k in range(slots):
                total = total + terms[k] * jnp.where(hits[k] == r, 1.0, 0.0)
            near[r * tile : (r + 1) * tile, :] = total

    for l in range(levels):
        loads[f"self{l}"].wait()
        sums = [cmul(own[l, 0], own[l, 1], coef[l, c]) for c in range(CHUNKS)]
        if l + 1 == levels:
            send_beside(edge)
            near_field()
        loads[f"cross{l}"].wait()
        for c in range(CHUNKS):
            copies[l, c].wait_recv()
            after = (sums[c] + cmul(cross[l, 0], cross[l, 1], got[l, c])).astype(jnp.bfloat16)
            if l + 1 < levels:
                coef[l + 1, c] = after
                copies[l + 1, c] = exchange(l + 1, c)
                if c == 0:
                    until_ready(l + 1)
                copies[l + 1, c].start()
                continue
            if c == 0:
                loads["out"].wait()
            far = cmul(outb[0], outb[1], after)
            lo, hi = c * part, (c + 1) * part
            o_ref[0, :, lo:hi] = far[:, :part] + near[:, lo:hi]
            o_ref[1, :, lo:hi] = far[:, part:] + near[:, width + lo : width + hi]
    for copy in near_copies:
        copy.wait_send()
    for copy in copies.values():
        copy.wait_send()


def per_device(
    excitation, leaf_basis, self_transfer, cross_transfer, out_basis, near_tiles, near_list
):
    n = lax.axis_size("surf")
    rows, width = excitation.shape[1:]
    rank = leaf_basis.shape[1]
    levels = self_transfer.shape[0]
    slots, _, tile, _ = near_tiles.shape
    blocks = rows // tile
    by_slot = jnp.transpose(near_list, (1, 2, 0))
    half, full = jnp.bfloat16, jnp.float32
    anywhere = pl.BlockSpec(memory_space=pl.ANY)
    part = 2 * width // CHUNKS
    return pl.pallas_call(
        functools.partial(kernel, n),
        out_shape=pltpu.VMEM(excitation.shape, full),
        in_specs=[anywhere] * 7,
        out_specs=pl.BlockSpec(memory_space=pltpu.VMEM),
        scratch_shapes=[
            pltpu.VMEM(excitation.shape, full),
            pltpu.VMEM((blocks, tile, 2 * width), half),
            pltpu.VMEM((blocks + 4, tile, 2 * width), half),
            pltpu.VMEM(leaf_basis.shape, half),
            pltpu.VMEM(self_transfer.shape, half),
            pltpu.VMEM(cross_transfer.shape, half),
            pltpu.VMEM(out_basis.shape, half),
            pltpu.VMEM(near_tiles.shape, half),
            pltpu.SMEM(by_slot.shape, jnp.int32),
            pltpu.VMEM((2, 2, tile, 2 * width), half),
            pltpu.VMEM((2, 2, tile, 2 * width), half),
            pltpu.VMEM((levels, CHUNKS, rank, part), half),
            pltpu.VMEM((levels, CHUNKS, rank, part), half),
            pltpu.VMEM((slots, tile, 2 * width), full),
            pltpu.VMEM((rows, 2 * width), full),
            pltpu.SemaphoreType.DMA((5 + 2 * levels,)),
            pltpu.SemaphoreType.DMA((2,)),
            pltpu.SemaphoreType.DMA((2,)),
            pltpu.SemaphoreType.DMA((levels, CHUNKS)),
            pltpu.SemaphoreType.DMA((levels, CHUNKS)),
            pltpu.SemaphoreType.REGULAR((levels + 1,)),
        ],
        compiler_params=pltpu.CompilerParams(
            collective_id=0, has_side_effects=True, vmem_limit_bytes=24 << 20
        ),
    )(
        *(
            pltpu.with_memory_space_constraint(array, pltpu.HBM)
            for array in (
                excitation,
                leaf_basis,
                self_transfer,
                cross_transfer,
                out_basis,
                near_tiles,
                by_slot,
            )
        )
    )


def solution(mesh):
    placed = (
        P(None, "surf", None),
        P(None, "surf", None),
        P(None, None, "surf", None),
        P(None, None, "surf", None),
        P(None, "surf", None),
        P("surf", None, None, None),
        P(),
    )
    return jax.shard_map(
        per_device, mesh=mesh, in_specs=placed, out_specs=P(None, "surf", None), check_vma=False
    )
```

```python
import functools

import jax
import jax.numpy as jnp
from jax import lax
from jax.experimental import pallas as pl
from jax.experimental.pallas import tpu as pltpu
from jax.sharding import PartitionSpec as P

MESH = pl.DeviceIdType.MESH
CUTS = (0, 128, 192, 256)
SHEET = 128


def cmul(real, imag, block):
    half = block.shape[-1] // 2
    plain = jnp.dot(real, block, preferred_element_type=jnp.float32)
    if half % 128 == 0:
        turned = jnp.concatenate([-block[:, half:], block[:, :half]], axis=1)
        return plain + jnp.dot(imag, turned, preferred_element_type=jnp.float32)
    other = pltpu.roll(jnp.dot(imag, block, preferred_element_type=jnp.float32), half, 1)
    lane = lax.broadcasted_iota(jnp.int32, other.shape, 1)
    return plain + jnp.where(lane < half, -other, other)


def kernel(
    n,
    x_hbm,
    leaf_hbm,
    self_hbm,
    cross_hbm,
    out_hbm,
    tiles_hbm,
    list_hbm,
    o_ref,
    xf,
    xb,
    window,
    leaf,
    own,
    cross,
    outb,
    tiles,
    listed,
    near_send,
    near_recv,
    terms,
    near,
    load_sem,
    near_ssem,
    near_rsem,
    send_sem,
    recv_sem,
    ready,
    *traded,
):
    me = lax.axis_index("surf")
    levels = own.shape[0]
    blocks, tile, wide = xb.shape
    width = wide // 2
    chunks = len(CUTS) - 1
    coef, got = traded[:chunks], traded[chunks:]
    slots = tiles.shape[0]
    group = 1 << levels

    def parity(device):
        return lax.rem(sum(lax.rem(device // (1 << l), 2) for l in range(levels)), 2)

    odd = lax.rem(me, 2)
    left = lax.rem(me + n - 1, n)
    right = lax.rem(me + 1, n)
    mate = me ^ 1
    beside = lax.rem(me + n - 1 + 2 * odd, n)
    place = lax.rem(me, group)
    last_side = levels
    hub = parity(me) == 0
    answers_beside = odd == 1
    barrier = pltpu.get_barrier_semaphore()

    def greet(device):
        pl.semaphore_signal(barrier, inc=1, device_id=(device,), device_id_type=MESH)

    def answer(device, which):
        pl.semaphore_signal(ready.at[which], inc=1, device_id=(device,), device_id_type=MESH)

    @pl.when(jnp.logical_not(hub))
    def _():
        for l in range(levels):
            greet(me ^ (1 << l))

    @pl.when(jnp.logical_not(answers_beside))
    def _():
        greet(beside)

    loads = {}

    def load(name, src, dst):
        loads[name] = pltpu.make_async_copy(src, dst, load_sem.at[len(loads)])
        loads[name].start()

    for b in range(blocks):
        rows = pl.ds(b * tile, tile)
        load(f"x{b}", x_hbm.at[:, rows], xf.at[:, rows])
    load("list", list_hbm, listed)
    load("leaf", leaf_hbm, leaf)

    def until_ready(level):
        @pl.when(jnp.logical_not(hub))
        def _():
            pl.semaphore_wait(ready.at[level], 1)

    for b in range(blocks):
        loads[f"x{b}"].wait()
        rows = slice(b * tile, (b + 1) * tile)
        both = jnp.concatenate([xf[0, rows, :], xf[1, rows, :]], axis=1).astype(jnp.bfloat16)
        xb[b] = both

    for l in range(levels):
        load(f"self{l}", self_hbm.at[l], own.at[l])
        load(f"cross{l}", cross_hbm.at[l], cross.at[l])
    load("tiles", tiles_hbm, tiles)
    load("out", out_hbm, outb)

    @pl.when(jnp.logical_and(hub, answers_beside))
    def _():
        pl.semaphore_wait(barrier, levels + 1)

    @pl.when(jnp.logical_and(hub, jnp.logical_not(answers_beside)))
    def _():
        pl.semaphore_wait(barrier, levels)

    @pl.when(jnp.logical_and(jnp.logical_not(hub), answers_beside))
    def _():
        pl.semaphore_wait(barrier, 1)

    @pl.when(hub)
    def _():
        for l in range(levels):
            answer(me ^ (1 << l), l)

    @pl.when(answers_beside)
    def _():
        answer(beside, last_side)

    def chunk(c):
        lo, hi = CUTS[c], CUTS[c + 1]
        rows = blocks * tile
        real = xb[:, :, lo:hi].reshape(rows, hi - lo)
        imag = xb[:, :, width + lo : width + hi].reshape(rows, hi - lo)
        return jnp.concatenate([real, imag], axis=1)

    def exchange(level, c):
        return pltpu.make_async_remote_copy(
            src_ref=coef[c].at[level],
            dst_ref=got[c].at[level],
            send_sem=send_sem.at[level, c],
            recv_sem=recv_sem.at[level, c],
            device_id=(me ^ (1 << level),),
            device_id_type=MESH,
        )

    def listed_span(patch, owner):
        low, high = jnp.int32(blocks), jnp.int32(-1)
        for k in range(slots):
            hit = listed[k, 0, patch] == owner
            col = listed[k, 2, patch]
            low = jnp.minimum(low, jnp.where(hit, col, blocks))
            high = jnp.maximum(high, jnp.where(hit, col, -1))
        return jnp.where(high < 0, 0, low), jnp.maximum(high, 0)

    def near_copy(side, device):
        return pltpu.make_async_remote_copy(
            src_ref=near_send.at[side],
            dst_ref=near_recv.at[side],
            send_sem=near_ssem.at[side],
            recv_sem=near_rsem.at[side],
            device_id=(device,),
            device_id_type=MESH,
        )

    near_copies = [near_copy(0, mate), near_copy(1, beside)]

    def send_near(side, device):
        low, high = listed_span(device, me)
        near_send[side, 0] = xb[low]
        near_send[side, 1] = xb[high]
        near_copies[side].start()

    def send_beside(when):
        @pl.when(when)
        def _():
            @pl.when(jnp.logical_not(answers_beside))
            def _():
                pl.semaphore_wait(ready.at[last_side], 1)

            send_near(1, beside)

    first = place == 0
    edge = lax.rem(me, SHEET) == 0
    loads["list"].wait()
    send_beside(jnp.logical_not(first))

    loads["leaf"].wait()
    copies = {}
    for c in range(chunks):
        coef[c][0] = cmul(leaf[0], leaf[1], chunk(c)).astype(jnp.bfloat16)
        copies[0, c] = exchange(0, c)
        if c == 0:
            until_ready(0)
        copies[0, c].start()
    send_near(0, mate)
    send_beside(jnp.logical_and(first, jnp.logical_not(edge)))

    def near_field():
        loads["tiles"].wait()
        for copy in near_copies:
            copy.wait_recv()
        for b in range(blocks):
            window[b] = xb[b]
        for s in range(2):
            for h in range(2):
                window[blocks + 2 * s + h] = near_recv[s, h]
        low_mate, _ = listed_span(me, mate)
        low_beside, _ = listed_span(me, beside)
        hits = []
        for k in range(slots):
            owner, row, col = listed[k, 0, me], listed[k, 1, me], listed[k, 2, me]
            at = jnp.where(
                owner == mate,
                blocks + (col != low_mate).astype(jnp.int32),
                jnp.where(owner == beside, blocks + 2 + (col != low_beside).astype(jnp.int32), col),
            )
            hits.append(jnp.where(owner >= 0, row, -1))
            terms[k] = cmul(tiles[k, 0], tiles[k, 1], window[at])
        for r in range(blocks):
            total = jnp.zeros((tile, wide), jnp.float32)
            for k in range(slots):
                total = total + terms[k] * jnp.where(hits[k] == r, 1.0, 0.0)
            near[r * tile : (r + 1) * tile, :] = total

    for l in range(levels):
        loads[f"self{l}"].wait()
        sums = [cmul(own[l, 0], own[l, 1], coef[c][l]) for c in range(chunks)]
        if l + 1 == levels:
            send_beside(edge)
            near_field()
        loads[f"cross{l}"].wait()
        for c in range(chunks):
            copies[l, c].wait_recv()
            after = (sums[c] + cmul(cross[l, 0], cross[l, 1], got[c][l])).astype(jnp.bfloat16)
            if l + 1 < levels:
                coef[c][l + 1] = after
                copies[l + 1, c] = exchange(l + 1, c)
                if c == 0:
                    until_ready(l + 1)
                copies[l + 1, c].start()
                continue
            if c == 0:
                loads["out"].wait()
            far = cmul(outb[0], outb[1], after)
            lo, hi = CUTS[c], CUTS[c + 1]
            part = hi - lo
            o_ref[0, :, lo:hi] = far[:, :part] + near[:, lo:hi]
            o_ref[1, :, lo:hi] = far[:, part:] + near[:, width + lo : width + hi]
    for copy in near_copies:
        copy.wait_send()
    for copy in copies.values():
        copy.wait_send()


def per_device(
    excitation, leaf_basis, self_transfer, cross_transfer, out_basis, near_tiles, near_list
):
    n = lax.axis_size("surf")
    rows, width = excitation.shape[1:]
    rank = leaf_basis.shape[1]
    levels = self_transfer.shape[0]
    slots, _, tile, _ = near_tiles.shape
    blocks = rows // tile
    by_slot = jnp.transpose(near_list, (1, 2, 0))
    half, full = jnp.bfloat16, jnp.float32
    anywhere = pl.BlockSpec(memory_space=pl.ANY)
    traded = [
        pltpu.VMEM((levels, rank, 2 * (hi - lo)), half) for lo, hi in zip(CUTS, CUTS[1:])
    ]
    return pl.pallas_call(
        functools.partial(kernel, n),
        out_shape=pltpu.VMEM(excitation.shape, full),
        in_specs=[anywhere] * 7,
        out_specs=pl.BlockSpec(memory_space=pltpu.VMEM),
        scratch_shapes=[
            pltpu.VMEM(excitation.shape, full),
            pltpu.VMEM((blocks, tile, 2 * width), half),
            pltpu.VMEM((blocks + 4, tile, 2 * width), half),
            pltpu.VMEM(leaf_basis.shape, half),
            pltpu.VMEM(self_transfer.shape, half),
            pltpu.VMEM(cross_transfer.shape, half),
            pltpu.VMEM(out_basis.shape, half),
            pltpu.VMEM(near_tiles.shape, half),
            pltpu.SMEM(by_slot.shape, jnp.int32),
            pltpu.VMEM((2, 2, tile, 2 * width), half),
            pltpu.VMEM((2, 2, tile, 2 * width), half),
            pltpu.VMEM((slots, tile, 2 * width), full),
            pltpu.VMEM((rows, 2 * width), full),
            pltpu.SemaphoreType.DMA((4 + blocks + 2 * levels,)),
            pltpu.SemaphoreType.DMA((2,)),
            pltpu.SemaphoreType.DMA((2,)),
            pltpu.SemaphoreType.DMA((levels, len(traded))),
            pltpu.SemaphoreType.DMA((levels, len(traded))),
            pltpu.SemaphoreType.REGULAR((levels + 1,)),
            *traded,
            *traded,
        ],
        compiler_params=pltpu.CompilerParams(
            collective_id=0, has_side_effects=True, vmem_limit_bytes=24 << 20
        ),
    )(
        *(
            pltpu.with_memory_space_constraint(array, pltpu.HBM)
            for array in (
                excitation,
                leaf_basis,
                self_transfer,
                cross_transfer,
                out_basis,
                near_tiles,
                by_slot,
            )
        )
    )


def solution(mesh):
    placed = (
        P(None, "surf", None),
        P(None, "surf", None),
        P(None, None, "surf", None),
        P(None, None, "surf", None),
        P(None, "surf", None),
        P("surf", None, None, None),
        P(),
    )
    return jax.shard_map(
        per_device, mesh=mesh, in_specs=placed, out_specs=P(None, "surf", None), check_vma=False
    )
```
